32 devices in a mesh: ctx: 8 (over z, y), ch: 4 (over x, core).
Axes of the slice: x: 2, y: 2, z: 4, core: 2. Of those that a mesh axis runs over, the one named last changes fastest.
Arguments:
- query: bfloat16 [32768, 512], P('ctx', 'ch'), parts along dimension 1, may hold values from -6 to 6
- key_proj: bfloat16 [32768, 512], P('ctx', 'ch'), parts along dimension 1, may hold values from -6 to 6
- value: bfloat16 [32768, 512], P('ctx', 'ch'), parts along dimension 1, may hold values from -6 to 6
- short_taps: float32 [3, 3, 512], P(None, None, 'ch'), parts along dimension 2, may hold values from -3.5 to 3.5
- bias: float32 [512], P('ch'), parts along dimension 0, may hold values from -4 to 4
- long_filter: bfloat16 [32768, 512], P('ctx', 'ch'), parts along dimension 1, may hold values from -0.03125 to 0.03125
Outputs:
- gated: bfloat16 [32768, 512], P('ctx', 'ch'), parts along dimension 1
The draws below stay inside these ranges and needn't reach their ends.
There are 4 independent parts, one for each index of `ch`. The reference program is written for one: setup_inputs(seed, part) draws one part's arguments, and reference() takes and returns one part's arrays. A program takes and returns all parts, laid end to end along the dimension named above; each array names one. Nothing has to cross between parts.
All inputs are finite; a program needn't handle non-finite values.
Results may differ from the reference program's by a relative error of at most 0.006.
Values may be sent and summed in bfloat16 or wider, within the bound.
A program may use at most 128 MiB of HBM per device.

```python
import jax
import jax.numpy as jnp
from jax import lax

C = 128
SHORT = 3
SEQ = 32768


def block_levels(stream_key, shape, cuts, low, largest):
    level, own = 1.0, jax.random.fold_in(stream_key, 6)
    for position, parts in cuts:
        draws = jnp.exp(jax.random.uniform(jax.random.fold_in(own, position), (parts,), jnp.float32, low / len(cuts), largest / len(cuts)))
        level = level * jnp.repeat(draws, shape[position] // parts).reshape([-1 if axis == position else 1 for axis in range(len(shape))])
    return level


def bell_draw(key, extent, spread, bound, pieces=(), held_as=jnp.bfloat16):
    array = spread * jax.random.normal(key, extent, jnp.float32)
    if pieces:
        array = array * block_levels(key, extent, pieces, -0.22, 0.18)
    return jnp.clip(array, -bound, bound).astype(held_as)


def setup_inputs(seed: int = 0, part: int = 0) -> dict:
    splits = jax.random.split(jax.random.key(seed), 7)
    part_splits = jax.random.split(jax.random.fold_in(splits[6], part), 7)
    return {
        "query": bell_draw(part_splits[0], (SEQ, C), 1.0, 6.0, ((0, 8),)),
        "key_proj": bell_draw(part_splits[1], (SEQ, C), 1.0, 6.0, ((0, 8),)),
        "value": bell_draw(part_splits[2], (SEQ, C), 1.0, 6.0, ((0, 8),)),
        "short_taps": bell_draw(part_splits[3], (3, SHORT, C), SHORT ** -0.5, 3.5, (), jnp.float32),
        "bias": bell_draw(part_splits[4], (C,), 1.0, 4.0, (), jnp.float32),
        "long_filter": bell_draw(part_splits[5], (SEQ, C), SEQ ** -0.5, 0.03125, ((0, 8),)),
    }


def featurize(stream, taps):
    width = stream.shape[1]
    padded = jnp.concatenate([jnp.zeros((SHORT - 1, width), stream.dtype), stream], axis=0)
    total = jnp.zeros(stream.shape, jnp.float32)
    for offset in range(SHORT):
        total = total + taps[offset] * padded[SHORT - 1 - offset:SHORT - 1 - offset + SEQ].astype(jnp.float32)
    return total


def reference(query, key_proj, value, short_taps, bias, long_filter):
    query_feat = featurize(query, short_taps[0]).astype(jnp.bfloat16)
    query_wide = lax.optimization_barrier(query_feat).astype(jnp.float32)
    mixed = (featurize(key_proj, short_taps[1]) * featurize(value, short_taps[2])).astype(jnp.bfloat16)
    mixed_wide = lax.optimization_barrier(mixed).astype(jnp.float32)
    filter_wide = long_filter.astype(jnp.float32)
    spectrum = jnp.fft.rfft(mixed_wide, n=2 * SEQ, axis=0) * jnp.fft.rfft(filter_wide, n=2 * SEQ, axis=0)
    convolved = jnp.fft.irfft(spectrum, n=2 * SEQ, axis=0)[:SEQ].astype(jnp.bfloat16)
    convolved = lax.optimization_barrier(convolved).astype(jnp.float32)
    return (query_wide * (convolved + bias * mixed_wide)).astype(jnp.bfloat16)
```

```python
import functools

import jax
import jax.numpy as jnp
import numpy as np
from jax import lax
from jax.experimental import pallas as pl
from jax.experimental.pallas import tpu as pltpu
from jax.sharding import PartitionSpec as P

BF = jnp.bfloat16
F32 = jnp.float32
CHUNKS = 4
PAD = 8
MESH = pl.DeviceIdType.MESH


def halves(table):
    table = np.asarray(table, np.float32)
    high = table.astype(jnp.bfloat16)
    return high, (table - high.astype(np.float32)).astype(jnp.bfloat16)


def make_tables(parts, high, mid, fold, width):
    group = width // fold
    first = parts * high
    n = first * mid * fold
    s = np.arange(first)
    lane = np.arange(fold)
    angle = 2 * np.pi * ((np.outer(s, 4 * s + 1) % (4 * first)) / (4 * first))
    into = np.concatenate([np.cos(angle.T), -np.sin(angle.T)], axis=0)
    back = np.concatenate([np.cos(angle), -np.sin(angle)], axis=1) / n
    f = np.arange(mid)[:, None, None] * fold + np.repeat(lane, group)[None, None, :]
    turn = np.exp(-2j * np.pi * f * (s[None, :, None] + 0.25) / n)
    turn = np.stack([turn.real, turn.imag], axis=1).astype(np.float32)
    right, left = [], []
    for c in range(mid):
        w = np.exp(-2j * np.pi * (np.outer(lane, np.full(fold, c)) / (mid * fold) + np.outer(lane, lane) / fold))
        w = np.kron(w, np.eye(group))
        right.append(np.block([[w.real, w.imag], [-w.imag, w.real]]))
        v = w.conj().T
        left.append(np.block([[v.real, v.imag], [-v.imag, v.real]]))
    into_h, into_l = halves(into)
    right_h, right_l = halves(np.stack(right))
    return (
        np.concatenate([into_h, into_l], axis=0),
        back.astype(jnp.bfloat16),
        turn,
        right_h,
        right_l,
        np.stack(left).astype(jnp.bfloat16),
    )


def dot(a, b):
    return jnp.dot(a, b, preferred_element_type=F32)


def small_dft(xs, sign):
    count = len(xs)
    if count == 1:
        return xs
    even = small_dft(xs[0::2], sign)
    odd = small_dft(xs[1::2], sign)
    out = [None] * count
    for k in range(count // 2):
        re, im = odd[k]
        angle = sign * 2 * np.pi * k / count
        c, s = float(np.cos(angle)), float(np.sin(angle))
        if k == 0:
            tr, ti = re, im
        elif 4 * k == count:
            tr, ti = (-im, re) if sign > 0 else (im, -re)
        else:
            tr, ti = re * c - im * s, re * s + im * c
        er, ei = even[k]
        out[k] = (er + tr, ei + ti)
        out[k + count // 2] = (er - tr, ei - ti)
    return out


def regroup(xs, fold, width):
    group = width // fold
    lane = lax.broadcasted_iota(jnp.int32, xs[0].shape, 1) // group
    xs = [pltpu.roll(x, i * group, 1) if i else x for i, x in enumerate(xs)]
    bit = 1
    while bit < fold:
        take = (lane // bit) % 2 == 1
        xs = [jnp.where(take, xs[(m + bit) % fold], xs[m]) for m in range(fold)]
        bit *= 2
    out = [xs[(fold - e) % fold] for e in range(fold)]
    return [pltpu.roll(x, width - e * group, 1) if e else x for e, x in enumerate(out)]


def body(
    parts, high, mid, fold, width,
    q_hbm, k_hbm, v_hbm, taps, bias, f_hbm, into_hbm, back_hbm, turn_hbm, right_h_hbm, right_l_hbm, left_hbm, o_ref,
    q_in, k_in, v_in, f_in, into, back, turn, right_h, right_l, left, loaded,
    halo, mixed, q_feat, wide, out_f, out_m, out_y, in_f, in_m, in_y,
    mid_a, z_h, z_l, spectrum, gathered,
    send, recv, own, send_f, recv_f, own_f, halo_send, halo_recv,
):
    me = lax.axis_index("ctx")
    chunks = fold // parts
    first = parts * high
    block = mid * fold
    pitch = block + PAD
    length = high * block
    count = taps.shape[1]
    streams = (q_in, k_in, v_in)

    barrier = pltpu.get_barrier_semaphore()

    def greet(k, carry):
        pl.semaphore_signal(barrier, inc=1, device_id={"ctx": lax.rem(me + k, parts)}, device_id_type=MESH)
        return carry

    lax.fori_loop(1, parts, greet, 0)

    pairs = (
        (f_hbm, f_in), (k_hbm, k_in), (v_hbm, v_in), (q_hbm, q_in), (into_hbm, into), (turn_hbm, turn),
        (right_h_hbm, right_h), (right_l_hbm, right_l), (left_hbm, left), (back_hbm, back),
    )
    loads = [pltpu.make_async_copy(a, b, loaded.at[i]) for i, (a, b) in enumerate(pairs)]
    for load in loads:
        load.start()

    def filter_copy(r, there, slot, source):
        return pltpu.make_async_remote_copy(
            src_ref=out_f.at[r, there],
            dst_ref=in_f.at[r, slot],
            send_sem=send_f.at[r, there],
            recv_sem=recv_f.at[r, source],
            device_id={"ctx": there},
            device_id_type=MESH,
        )

    outs = (out_m, out_y)
    ins = (in_m, in_y)

    def remote(kind, g, there, slot, source):
        return pltpu.make_async_remote_copy(
            src_ref=outs[kind].at[g, there],
            dst_ref=ins[kind].at[g, slot],
            send_sem=send.at[kind, g, there],
            recv_sem=recv.at[kind, g, source],
            device_id={"ctx": there},
            device_id_type=MESH,
        )

    def every(go):
        def step(k, carry):
            go(lax.rem(me + k, parts))
            return carry

        lax.fori_loop(1, parts, step, 0)

    def local_copy(kind, g):
        return pltpu.make_async_copy(outs[kind].at[g, me], ins[kind].at[g, me], own.at[kind, g])

    def local_filter(r):
        return pltpu.make_async_copy(out_f.at[r, me], in_f.at[r, me], own_f.at[r])

    def start(kind, g):
        every(lambda there: remote(kind, g, there, me, me).start())
        local_copy(kind, g).start()

    def wait(kind, g):
        every(lambda there: remote(kind, g, there, there, there).wait_recv())
        local_copy(kind, g).wait()

    def halo_copy(s):
        return pltpu.make_async_remote_copy(
            src_ref=streams[s].at[pl.ds(length - 16, 16)],
            dst_ref=halo.at[s],
            send_sem=halo_send.at[s],
            recv_sem=halo_recv.at[s],
            device_id={"ctx": lax.rem(me + 1, parts)},
            device_id_type=MESH,
        )

    rows = 64
    per_block = block // rows

    def wide_at(i):
        return pl.ds(pl.multiple_of((i // per_block) * pitch + (i % per_block) * rows, 8), rows)

    def rows_at(i):
        return pl.ds(pl.multiple_of(i * rows, rows), rows)

    tile = 16

    def pack_rows(r, store):
        def step(i, carry):
            xs = [wide[pl.ds(i * tile * pitch + r * fold + l, tile, stride=pitch), :] for l in range(fold)]
            store(pl.ds(pl.multiple_of(i * tile, tile), tile), regroup(xs, fold, width))
            return carry

        lax.fori_loop(0, high // tile, step, 0)

    loads[0].wait()

    def widen(i, carry):
        wide[wide_at(i), :] = f_in[rows_at(i), :].astype(F32)
        return carry

    lax.fori_loop(0, length // rows, widen, 0)

    def pack_filter(r, carry):
        def store(at, moved):
            for e in range(fold):
                out_f[r, e // chunks, e % chunks, at, :] = moved[e].astype(BF)

        pack_rows(r, store)
        return carry

    pack_filter(0, 0)
    pl.semaphore_wait(barrier, parts - 1)

    def send_filter(r, carry):
        every(lambda there: filter_copy(r, there, me, me).start())
        local_filter(r).start()
        return carry

    send_filter(0, 0)

    def more_filter(r, carry):
        pack_filter(r, 0)
        return send_filter(r, 0)

    lax.fori_loop(1, mid, more_filter, 0)

    for load in loads[1:4]:
        load.wait()
    for s in range(3):
        halo_copy(s).start()
    for s in range(3):
        halo_copy(s).wait_recv()
    inside = jnp.where(me == 0, 0.0, 1.0).astype(F32)

    def shifted(x_ref, s, i, tail):
        now = x_ref[rows_at(i), :].astype(F32)
        extended = jnp.concatenate([tail, now], axis=0)
        total = taps[s, 0][None] * now
        for j in range(1, count):
            total = total + taps[s, j][None] * pltpu.roll(extended, j, 0)[8:]
        return total, now[rows - 8 :]

    tails = [halo[s].astype(F32)[8:] * inside for s in range(3)]

    def features(i, carry):
        key, key_tail = shifted(k_in, 1, i, carry[0])
        val, val_tail = shifted(v_in, 2, i, carry[1])
        product = (key * val).astype(BF)
        mixed[rows_at(i), :] = product
        wide[wide_at(i), :] = product.astype(F32)
        return key_tail, val_tail

    lax.fori_loop(0, length // rows, features, (tails[1], tails[2]))

    def pack_mixed(r, carry):
        def store(at, moved):
            for e in range(fold):
                out_m[e % chunks, e // chunks, r, at, :] = moved[e].astype(BF)

        pack_rows(r, store)
        return carry

    lax.fori_loop(0, mid, pack_mixed, 0)
    for g in range(chunks):
        start(0, g)

    def q_features(i, carry):
        total, tail = shifted(q_in, 0, i, carry)
        q_feat[rows_at(i), :] = total.astype(BF)
        return tail

    lax.fori_loop(0, length // rows, q_features, tails[0])

    def twist(i, carry):
        at = pl.ds(pl.multiple_of(i * tile, tile), tile)
        low = pl.ds(pl.multiple_of(first + i * tile, tile), tile)
        xs = []
        for r in range(mid):
            re = mid_a[at, r * width : (r + 1) * width]
            im = mid_a[low, r * width : (r + 1) * width]
            tr, ti = turn[r, 0, at, :], turn[r, 1, at, :]
            xs.append((re * tr - im * ti, re * ti + im * tr))
        for c, pair in enumerate(small_dft(xs, -1)):
            for e in range(2):
                high_part = pair[e].astype(BF)
                z_h[c, at, e * width : (e + 1) * width] = high_part
                z_l[c, at, e * width : (e + 1) * width] = (pair[e] - high_part.astype(F32)).astype(BF)
        return carry

    def untwist(i, carry):
        at = pl.ds(pl.multiple_of(i * tile, tile), tile)
        low = pl.ds(pl.multiple_of(first + i * tile, tile), tile)
        xs = [(gathered[c, at, 0:width], gathered[c, at, width:]) for c in range(mid)]
        for r, (re, im) in enumerate(small_dft(xs, 1)):
            tr, ti = turn[r, 0, at, :], turn[r, 1, at, :]
            z_l[r // 2, at, (r % 2) * width : (r % 2 + 1) * width] = (re * tr + im * ti).astype(BF)
            z_h[r // 2, at, (r % 2) * width : (r % 2 + 1) * width] = (im * tr - re * ti).astype(BF)
        return carry

    def forward(source):
        for p in range(mid // 2):
            x = jnp.concatenate([source(2 * p), source(2 * p + 1)], axis=1)
            t = dot(into[...], x)
            mid_a[:, 2 * p * width : (2 * p + 2) * width] = t[: 2 * first] + t[2 * first :]
        lax.fori_loop(0, first // tile, twist, 0, unroll=2)

    def fine(c):
        top = z_h[c]
        return dot(top, right_h[c]) + dot(top, right_l[c]) + dot(z_l[c], right_h[c])

    for load in loads[4:]:
        load.wait()

    def arrive_filter(r, carry):
        every(lambda there: filter_copy(r, there, there, there).wait_recv())
        local_filter(r).wait()
        return carry

    lax.fori_loop(0, mid, arrive_filter, 0)

    def filter_chunk(g, carry):
        forward(lambda r: in_f[r, :, g].reshape(first, width))
        for c in range(mid):
            spectrum[g, c] = fine(c)
        return carry

    lax.fori_loop(0, chunks, filter_chunk, 0)

    def chunk(g, carry):
        wait(0, g)
        forward(lambda r: in_m[g, :, r].reshape(first, width))
        for c in range(mid):
            x = fine(c)
            h = spectrum[g, c]
            xr, xi, hr, hi = x[:, :width], x[:, width:], h[:, :width], h[:, width:]
            product = jnp.concatenate([xr * hr - xi * hi, xr * hi + xi * hr], axis=1).astype(BF)
            gathered[c] = dot(product, left[c])
        lax.fori_loop(0, first // tile, untwist, 0, unroll=2)
        for p in range(mid // 2):
            y = dot(back[:, :first], z_l[p]) + dot(back[:, first:], z_h[p])
            y = y.astype(BF)
            for e in range(2):
                out_y[g, :, 2 * p + e] = y[:, e * width : (e + 1) * width].reshape(parts, high, width)
        start(1, g)
        return carry

    lax.fori_loop(0, chunks, chunk, 0)

    def arrive(g, carry):
        wait(1, g)
        return carry

    lax.fori_loop(0, chunks, arrive, 0)

    def unpack(r, carry):
        def step(i, inner):
            at = pl.ds(pl.multiple_of(i * tile, tile), tile)
            xs = [in_y[e % chunks, e // chunks, r, at, :].astype(F32) for e in range(fold)]
            for l, x in enumerate(regroup(xs, fold, width)):
                wide[pl.ds(i * tile * pitch + r * fold + l, tile, stride=pitch), :] = x
            return inner

        lax.fori_loop(0, high // tile, step, 0)
        return carry

    lax.fori_loop(0, mid, unpack, 0)

    def gate(i, carry):
        at = rows_at(i)
        total = wide[wide_at(i), :] + bias[...] * mixed[at, :].astype(F32)
        o_ref[at, :] = (q_feat[at, :].astype(F32) * total).astype(BF)
        return carry

    lax.fori_loop(0, length // rows, gate, 0)

    for s in range(3):
        halo_copy(s).wait_send()

    def drain_filter(r, carry):
        every(lambda there: filter_copy(r, there, me, me).wait_send())
        return carry

    lax.fori_loop(0, mid, drain_filter, 0)

    def drain(g, carry):
        for kind in range(2):
            every(lambda there: remote(kind, g, there, me, me).wait_send())
        return carry

    lax.fori_loop(0, chunks, drain, 0)


def local(query, key_proj, value, short_taps, bias, long_filter):
    length, width = query.shape
    parts = lax.axis_size("ctx")
    chunks = max(1, min(CHUNKS, width // (4 * parts)))
    fold = parts * chunks
    high = max(16, 256 // parts)
    mid = length // (fold * high)
    first = parts * high
    tables = make_tables(parts, high, mid, fold, width)
    rows = pltpu.VMEM((length, width), BF)
    by_row = pltpu.VMEM((mid, parts, chunks, high, width), BF)
    by_chunk = pltpu.VMEM((chunks, parts, mid, high, width), BF)
    tall = pltpu.VMEM((mid, first, 2 * width), BF)
    vmem = pl.BlockSpec(memory_space=pltpu.VMEM)
    hbm = pl.BlockSpec(memory_space=pl.ANY)
    return pl.pallas_call(
        functools.partial(body, parts, high, mid, fold, width),
        out_shape=jax.ShapeDtypeStruct((length, width), BF),
        in_specs=[hbm, hbm, hbm, vmem, vmem, hbm] + [hbm] * 6,
        out_specs=vmem,
        scratch_shapes=[
            rows, rows, rows, rows,
            *[pltpu.VMEM(t.shape, t.dtype) for t in tables],
            pltpu.SemaphoreType.DMA((10,)),
            pltpu.VMEM((3, 16, width), BF),
            rows, rows,
            pltpu.VMEM((high * (mid * fold + PAD), width), F32),
            by_row, by_chunk, by_chunk, by_row, by_chunk, by_chunk,
            pltpu.VMEM((2 * first, mid * width), F32),
            tall, tall,
            pltpu.VMEM((chunks, mid, first, 2 * width), F32),
            pltpu.VMEM((mid, first, 2 * width), F32),
            pltpu.SemaphoreType.DMA((2, chunks, parts)),
            pltpu.SemaphoreType.DMA((2, chunks, parts)),
            pltpu.SemaphoreType.DMA((2, chunks)),
            pltpu.SemaphoreType.DMA((mid, parts)),
            pltpu.SemaphoreType.DMA((mid, parts)),
            pltpu.SemaphoreType.DMA((mid,)),
            pltpu.SemaphoreType.DMA((3,)),
            pltpu.SemaphoreType.DMA((3,)),
        ],
        compiler_params=pltpu.CompilerParams(
            vmem_limit_bytes=56 * 1024 * 1024, collective_id=0, has_side_effects=True
        ),
    )(query, key_proj, value, short_taps, bias.reshape(1, width), long_filter, *tables)


def solution(mesh):
    in_specs = (
        P("ctx", "ch"),
        P("ctx", "ch"),
        P("ctx", "ch"),
        P(None, None, "ch"),
        P("ch"),
        P("ctx", "ch"),
    )
    return jax.shard_map(local, mesh=mesh, in_specs=in_specs, out_specs=P("ctx", "ch"), check_vma=False)
```

```python
import functools

import jax
import jax.numpy as jnp
import numpy as np
from jax import lax
from jax.experimental import pallas as pl
from jax.experimental.pallas import tpu as pltpu
from jax.sharding import PartitionSpec as P

BF = jnp.bfloat16
F32 = jnp.float32
CHUNKS = 4
PAD = 8
OUTS = 2
MESH = pl.DeviceIdType.MESH


def halves(table):
    table = np.asarray(table, np.float32)
    high = table.astype(jnp.bfloat16)
    return high, (table - high.astype(np.float32)).astype(jnp.bfloat16)


def make_tables(parts, high, mid, fold, width):
    group = width // fold
    first = parts * high
    n = first * mid * fold
    s = np.arange(first)
    lane = np.arange(fold)
    angle = 2 * np.pi * ((np.outer(s, 4 * s + 1) % (4 * first)) / (4 * first))
    into = np.concatenate([np.cos(angle.T), -np.sin(angle.T)], axis=0)
    back = np.concatenate([np.cos(angle), -np.sin(angle)], axis=1) / n
    f = np.arange(mid)[:, None, None] * fold + np.repeat(lane, group)[None, None, :]
    turn = np.exp(-2j * np.pi * f * (s[None, :, None] + 0.25) / n)
    turn = np.stack([turn.real, turn.imag], axis=1).astype(np.float32)
    right, left = [], []
    for c in range(mid):
        w = np.exp(-2j * np.pi * (np.outer(lane, np.full(fold, c)) / (mid * fold) + np.outer(lane, lane) / fold))
        w = np.kron(w, np.eye(group))
        right.append(np.block([[w.real, w.imag], [-w.imag, w.real]]))
        v = w.conj().T
        left.append(np.block([[v.real, v.imag], [-v.imag, v.real]]))
    into_h, into_l = halves(into)
    right_h, right_l = halves(np.stack(right))
    return (
        np.concatenate([into_h, into_l], axis=0),
        back.astype(jnp.bfloat16),
        turn,
        right_h,
        right_l,
        np.stack(left).astype(jnp.bfloat16),
    )


def dot(a, b):
    return jnp.dot(a, b, preferred_element_type=F32)


def small_dft(xs, sign):
    count = len(xs)
    if count == 1:
        return xs
    even = small_dft(xs[0::2], sign)
    odd = small_dft(xs[1::2], sign)
    out = [None] * count
    for k in range(count // 2):
        re, im = odd[k]
        angle = sign * 2 * np.pi * k / count
        c, s = float(np.cos(angle)), float(np.sin(angle))
        if k == 0:
            tr, ti = re, im
        elif 4 * k == count:
            tr, ti = (-im, re) if sign > 0 else (im, -re)
        else:
            tr, ti = re * c - im * s, re * s + im * c
        er, ei = even[k]
        out[k] = (er + tr, ei + ti)
        out[k + count // 2] = (er - tr, ei - ti)
    return out


def select(xs, lane, bit, hop):
    take = (lane // bit) % 2 == 1
    return [jnp.where(take, xs[(m + hop) % len(xs)], x) for m, x in enumerate(xs)]


def combine(xs, chunk, chunks, group):
    lane = lax.broadcasted_iota(jnp.int32, xs[0].shape, 1) // group
    shifts = [(part * chunks + chunk) * group for part in range(len(xs))]
    xs = [pltpu.roll(x, shift, 1) if shift else x for x, shift in zip(xs, shifts)]
    hop = 1
    while hop < len(xs):
        xs = select(xs, lane, hop * chunks, hop)
        hop *= 2
    return xs


def spread(xs, chunks, group, width):
    fold = len(xs)
    lane = lax.broadcasted_iota(jnp.int32, xs[0].shape, 1) // group
    bit = 1
    while bit < chunks:
        xs = select(xs, lane, bit, bit)
        bit *= 2
    xs = [xs[(fold - e) % fold] for e in range(fold)]
    return [pltpu.roll(x, width - e * group, 1) if e else x for e, x in enumerate(xs)]


def regroup(xs, fold, width):
    group = width // fold
    return spread(combine(xs, 0, 1, group), 1, group, width)


def body(
    parts, high, mid, fold, width,
    q_hbm, k_hbm, v_hbm, taps_hbm, bias_hbm, f_hbm, into_hbm, back_hbm, turn_hbm, right_h_hbm, right_l_hbm, left_hbm, o_hbm,
    o_ref, stored,
    taps, bias, q_in, k_in, v_in, f_in, into, back, turn, right_h, right_l, left, loaded,
    halo, mixed, q_feat, wide, out_f, out_m, out_y, in_f, in_m, in_y,
    mid_a, z_h, z_l, spectrum, gathered,
    send, recv, own, send_f, recv_f, own_f, halo_send, halo_recv,
):
    me = lax.axis_index("ctx")
    chunks = fold // parts
    first = parts * high
    block = mid * fold
    pitch = block + PAD
    length = high * block
    count = taps.shape[1]
    streams = (q_in, k_in, v_in)

    barrier = pltpu.get_barrier_semaphore()

    def greet(k, carry):
        pl.semaphore_signal(barrier, inc=1, device_id={"ctx": lax.rem(me + k, parts)}, device_id_type=MESH)
        return carry

    lax.fori_loop(1, parts, greet, 0)

    pairs = (
        (f_hbm, f_in), (k_hbm, k_in), (v_hbm, v_in), (q_hbm, q_in), (taps_hbm, taps), (bias_hbm, bias), (into_hbm, into), (turn_hbm, turn),
        (right_h_hbm, right_h), (right_l_hbm, right_l), (left_hbm, left), (back_hbm, back),
    )
    loads = [pltpu.make_async_copy(a, b, loaded.at[i]) for i, (a, b) in enumerate(pairs)]
    for load in loads:
        load.start()

    def filter_copy(r, there, slot, source):
        return pltpu.make_async_remote_copy(
            src_ref=out_f.at[r, there],
            dst_ref=in_f.at[r, slot],
            send_sem=send_f.at[r, there],
            recv_sem=recv_f.at[r, source],
            device_id={"ctx": there},
            device_id_type=MESH,
        )

    outs = (out_m, out_y)
    ins = (in_m, in_y)

    def remote(kind, g, there, slot, source):
        return pltpu.make_async_remote_copy(
            src_ref=outs[kind].at[g, there],
            dst_ref=ins[kind].at[g, slot],
            send_sem=send.at[kind, g, there],
            recv_sem=recv.at[kind, g, source],
            device_id={"ctx": there},
            device_id_type=MESH,
        )

    def every(go):
        def step(k, carry):
            go(lax.rem(me + k, parts))
            return carry

        lax.fori_loop(1, parts, step, 0)

    def local_copy(kind, g):
        return pltpu.make_async_copy(outs[kind].at[g, me], ins[kind].at[g, me], own.at[kind, g])

    def local_filter(r):
        return pltpu.make_async_copy(out_f.at[r, me], in_f.at[r, me], own_f.at[r])

    def start(kind, g):
        every(lambda there: remote(kind, g, there, me, me).start())
        local_copy(kind, g).start()

    def wait(kind, g):
        every(lambda there: remote(kind, g, there, there, there).wait_recv())
        local_copy(kind, g).wait()

    def halo_copy(s):
        return pltpu.make_async_remote_copy(
            src_ref=streams[s].at[pl.ds(length - 16, 16)],
            dst_ref=halo.at[s],
            send_sem=halo_send.at[s],
            recv_sem=halo_recv.at[s],
            device_id={"ctx": lax.rem(me + 1, parts)},
            device_id_type=MESH,
        )

    rows = 64
    per_block = block // rows

    def wide_at(i):
        return pl.ds(pl.multiple_of((i // per_block) * pitch + (i % per_block) * rows, 8), rows)

    def rows_at(i):
        return pl.ds(pl.multiple_of(i * rows, rows), rows)

    tile = 16

    def pack_rows(r, store):
        def step(i, carry):
            xs = [wide[pl.ds(i * tile * pitch + r * fold + l, tile, stride=pitch), :] for l in range(fold)]
            store(pl.ds(pl.multiple_of(i * tile, tile), tile), regroup(xs, fold, width))
            return carry

        lax.fori_loop(0, high // tile, step, 0)

    loads[0].wait()

    def widen(i, carry):
        wide[wide_at(i), :] = f_in[rows_at(i), :].astype(F32)
        return carry

    lax.fori_loop(0, length // rows, widen, 0)

    def pack_filter(r, carry):
        def store(at, moved):
            for e in range(fold):
                out_f[r, e // chunks, e % chunks, at, :] = moved[e].astype(BF)

        pack_rows(r, store)
        return carry

    pack_filter(0, 0)
    pl.semaphore_wait(barrier, parts - 1)

    def send_filter(r, carry):
        every(lambda there: filter_copy(r, there, me, me).start())
        local_filter(r).start()
        return carry

    send_filter(0, 0)

    def more_filter(r, carry):
        pack_filter(r, 0)
        return send_filter(r, 0)

    lax.fori_loop(1, mid, more_filter, 0)

    for load in loads[1:6]:
        load.wait()
    for s in range(3):
        halo_copy(s).start()
    for s in range(3):
        halo_copy(s).wait_recv()
    inside = jnp.where(me == 0, 0.0, 1.0).astype(F32)

    def shifted(x_ref, s, i, tail):
        now = x_ref[rows_at(i), :].astype(F32)
        extended = jnp.concatenate([tail, now], axis=0)
        total = taps[s, 0][None] * now
        for j in range(1, count):
            total = total + taps[s, j][None] * pltpu.roll(extended, j, 0)[8:]
        return total, now[rows - 8 :]

    tails = [halo[s].astype(F32)[8:] * inside for s in range(3)]

    def features(i, carry):
        key, key_tail = shifted(k_in, 1, i, carry[0])
        val, val_tail = shifted(v_in, 2, i, carry[1])
        product = (key * val).astype(BF)
        mixed[rows_at(i), :] = product
        wide[wide_at(i), :] = product.astype(F32)
        return key_tail, val_tail

    lax.fori_loop(0, length // rows, features, (tails[1], tails[2]))

    def pack_mixed(r, carry):
        def store(at, moved):
            for e in range(fold):
                out_m[e % chunks, e // chunks, r, at, :] = moved[e].astype(BF)

        pack_rows(r, store)
        return carry

    lax.fori_loop(0, mid, pack_mixed, 0)
    for g in range(chunks):
        start(0, g)

    def q_features(i, carry):
        total, tail = shifted(q_in, 0, i, carry)
        q_feat[rows_at(i), :] = total.astype(BF)
        return tail

    lax.fori_loop(0, length // rows, q_features, tails[0])

    def twist(i, carry):
        at = pl.ds(pl.multiple_of(i * tile, tile), tile)
        low = pl.ds(pl.multiple_of(first + i * tile, tile), tile)
        xs = []
        for r in range(mid):
            re = mid_a[at, r * width : (r + 1) * width]
            im = mid_a[low, r * width : (r + 1) * width]
            tr, ti = turn[r, 0, at, :], turn[r, 1, at, :]
            xs.append((re * tr - im * ti, re * ti + im * tr))
        for c, pair in enumerate(small_dft(xs, -1)):
            for e in range(2):
                high_part = pair[e].astype(BF)
                z_h[c, at, e * width : (e + 1) * width] = high_part
                z_l[c, at, e * width : (e + 1) * width] = (pair[e] - high_part.astype(F32)).astype(BF)
        return carry

    def untwist(i, carry):
        at = pl.ds(pl.multiple_of(i * tile, tile), tile)
        low = pl.ds(pl.multiple_of(first + i * tile, tile), tile)
        xs = [(gathered[c, at, 0:width], gathered[c, at, width:]) for c in range(mid)]
        for r, (re, im) in enumerate(small_dft(xs, 1)):
            tr, ti = turn[r, 0, at, :], turn[r, 1, at, :]
            z_l[r // 2, at, (r % 2) * width : (r % 2 + 1) * width] = (re * tr + im * ti).astype(BF)
            z_h[r // 2, at, (r % 2) * width : (r % 2 + 1) * width] = (im * tr - re * ti).astype(BF)
        return carry

    def forward(source):
        for p in range(mid // 2):
            x = jnp.concatenate([source(2 * p), source(2 * p + 1)], axis=1)
            t = dot(into[...], x)
            mid_a[:, 2 * p * width : (2 * p + 2) * width] = t[: 2 * first] + t[2 * first :]
        lax.fori_loop(0, first // tile, twist, 0, unroll=2)

    def fine(c):
        top = z_h[c]
        return dot(top, right_h[c]) + dot(top, right_l[c]) + dot(z_l[c], right_h[c])

    for load in loads[6:]:
        load.wait()

    def arrive_filter(r, carry):
        every(lambda there: filter_copy(r, there, there, there).wait_recv())
        local_filter(r).wait()
        return carry

    lax.fori_loop(0, mid, arrive_filter, 0)

    def filter_chunk(g, carry):
        forward(lambda r: in_f[r, :, g].reshape(first, width))
        for c in range(mid):
            spectrum[g, c] = fine(c)
        return carry

    lax.fori_loop(0, chunks, filter_chunk, 0)

    def chunk(g, carry):
        wait(0, g)
        forward(lambda r: in_m[g, :, r].reshape(first, width))
        for c in range(mid):
            x = fine(c)
            h = spectrum[g, c]
            xr, xi, hr, hi = x[:, :width], x[:, width:], h[:, :width], h[:, width:]
            product = jnp.concatenate([xr * hr - xi * hi, xr * hi + xi * hr], axis=1).astype(BF)
            gathered[c] = dot(product, left[c])
        lax.fori_loop(0, first // tile, untwist, 0, unroll=2)
        for p in range(mid // 2):
            y = dot(back[:, :first], z_l[p]) + dot(back[:, first:], z_h[p])
            y = y.astype(BF)
            for e in range(2):
                out_y[g, :, 2 * p + e] = y[:, e * width : (e + 1) * width].reshape(parts, high, width)
        start(1, g)
        return carry

    lax.fori_loop(0, chunks, chunk, 0)

    group = width // fold
    tiles = high // tile

    def ready(g):
        def step(i, carry):
            r, at = i // tiles, pl.ds(pl.multiple_of(i % tiles * tile, tile), tile)
            xs = [in_y[g, part, r, at, :].astype(F32) for part in range(parts)]
            for part, x in enumerate(combine(xs, g, chunks, group)):
                in_y[g, part, r, at, :] = x.astype(BF)
            return carry

        lax.fori_loop(0, mid * tiles, step, 0)

    for s in range(3):
        halo_copy(s).wait_send()

    def drain_filter(r, carry):
        every(lambda there: filter_copy(r, there, me, me).wait_send())
        return carry

    lax.fori_loop(0, mid, drain_filter, 0)

    def drain(g, carry):
        every(lambda there: remote(0, g, there, me, me).wait_send())
        return carry

    lax.fori_loop(0, chunks, drain, 0)

    for g in range(chunks - 1):
        wait(1, g)
        ready(g)
        every(lambda there: remote(1, g, there, me, me).wait_send())
    wait(1, chunks - 1)

    def unpack(i, carry):
        r, k = i // tiles, i % tiles
        at = pl.ds(pl.multiple_of(k * tile, tile), tile)
        fresh = [in_y[chunks - 1, part, r, at, :].astype(F32) for part in range(parts)]
        fresh = combine(fresh, chunks - 1, chunks, group)
        xs = [
            fresh[e // chunks] if e % chunks == chunks - 1 else in_y[e % chunks, e // chunks, r, at, :].astype(F32)
            for e in range(fold)
        ]
        for l, x in enumerate(spread(xs, chunks, group, width)):
            wide[pl.ds(k * tile * pitch + r * fold + l, tile, stride=pitch), :] = x
        return carry

    lax.fori_loop(0, mid * tiles, unpack, 0)

    def gate(i, carry):
        at = rows_at(i)
        total = wide[wide_at(i), :] + bias[...] * mixed[at, :].astype(F32)
        o_ref[at, :] = (q_feat[at, :].astype(F32) * total).astype(BF)
        return carry

    stores = []
    span = length // OUTS
    for k in range(OUTS):
        lax.fori_loop(k * span // rows, (k + 1) * span // rows, gate, 0, unroll=4)
        at = pl.ds(k * span, span)
        stores.append(pltpu.make_async_copy(o_ref.at[at], o_hbm.at[at], stored.at[k]))
        stores[k].start()

    every(lambda there: remote(1, chunks - 1, there, me, me).wait_send())
    for store in stores:
        store.wait()


def local(query, key_proj, value, short_taps, bias, long_filter):
    length, width = query.shape
    parts = lax.axis_size("ctx")
    chunks = max(1, min(CHUNKS, width // (4 * parts)))
    fold = parts * chunks
    high = max(16, 256 // parts)
    mid = length // (fold * high)
    first = parts * high
    tables = make_tables(parts, high, mid, fold, width)
    rows = pltpu.VMEM((length, width), BF)
    by_row = pltpu.VMEM((mid, parts, chunks, high, width), BF)
    by_chunk = pltpu.VMEM((chunks, parts, mid, high, width), BF)
    tall = pltpu.VMEM((mid, first, 2 * width), BF)
    hbm = pl.BlockSpec(memory_space=pl.ANY)
    return pl.pallas_call(
        functools.partial(body, parts, high, mid, fold, width),
        out_shape=jax.ShapeDtypeStruct((length, width), BF),
        in_specs=[hbm] * 12,
        out_specs=hbm,
        scratch_shapes=[
            rows,
            pltpu.SemaphoreType.DMA((OUTS,)),
            pltpu.VMEM(short_taps.shape, F32),
            pltpu.VMEM((1, width), F32),
            rows, rows, rows, rows,
            *[pltpu.VMEM(t.shape, t.dtype) for t in tables],
            pltpu.SemaphoreType.DMA((12,)),
            pltpu.VMEM((3, 16, width), BF),
            rows, rows,
            pltpu.VMEM((high * (mid * fold + PAD), width), F32),
            by_row, by_chunk, by_chunk, by_row, by_chunk, by_chunk,
            pltpu.VMEM((2 * first, mid * width), F32),
            tall, tall,
            pltpu.VMEM((chunks, mid, first, 2 * width), F32),
            pltpu.VMEM((mid, first, 2 * width), F32),
            pltpu.SemaphoreType.DMA((2, chunks, parts)),
            pltpu.SemaphoreType.DMA((2, chunks, parts)),
            pltpu.SemaphoreType.DMA((2, chunks)),
            pltpu.SemaphoreType.DMA((mid, parts)),
            pltpu.SemaphoreType.DMA((mid, parts)),
            pltpu.SemaphoreType.DMA((mid,)),
            pltpu.SemaphoreType.DMA((3,)),
            pltpu.SemaphoreType.DMA((3,)),
        ],
        compiler_params=pltpu.CompilerParams(
            vmem_limit_bytes=56 * 1024 * 1024, collective_id=0, has_side_effects=True
        ),
    )(query, key_proj, value, short_taps, bias.reshape(1, width), long_filter, *tables)


def solution(mesh):
    in_specs = (
        P("ctx", "ch"),
        P("ctx", "ch"),
        P("ctx", "ch"),
        P(None, None, "ch"),
        P("ch"),
        P("ctx", "ch"),
    )
    return jax.shard_map(local, mesh=mesh, in_specs=in_specs, out_specs=P("ctx", "ch"), check_vma=False)
```

```python
import functools

import jax
import jax.numpy as jnp
import numpy as np
from jax import lax
from jax.experimental import pallas as pl
from jax.experimental.pallas import tpu as pltpu
from jax.sharding import PartitionSpec as P

BF = jnp.bfloat16
F32 = jnp.float32
CHUNKS = 4
PAD = 8
OUTS = 2
MESH = pl.DeviceIdType.MESH


def halves(table):
    table = np.asarray(table, np.float32)
    high = table.astype(jnp.bfloat16)
    return high, (table - high.astype(np.float32)).astype(jnp.bfloat16)


def make_tables(parts, high, mid, fold, width):
    group = width // fold
    first = parts * high
    n = first * mid * fold
    s = np.arange(first)
    lane = np.arange(fold)
    angle = 2 * np.pi * ((np.outer(s, 4 * s + 1) % (4 * first)) / (4 * first))
    into = np.concatenate([np.cos(angle.T), -np.sin(angle.T)], axis=0)
    back = np.concatenate([np.cos(angle), -np.sin(angle)], axis=1) / n
    f = np.arange(mid)[:, None, None] * fold + np.repeat(lane, group)[None, None, :]
    turn = np.exp(-2j * np.pi * f * (s[None, :, None] + 0.25) / n)
    turn = np.stack([turn.real, turn.imag], axis=1).astype(np.float32)
    right, left = [], []
    for c in range(mid):
        w = np.exp(-2j * np.pi * (np.outer(lane, np.full(fold, c)) / (mid * fold) + np.outer(lane, lane) / fold))
        w = np.kron(w, np.eye(group))
        right.append(np.block([[w.real, w.imag], [-w.imag, w.real]]))
        v = w.conj().T
        left.append(np.block([[v.real, v.imag], [-v.imag, v.real]]))
    into_h, into_l = halves(into)
    right_h, right_l = halves(np.stack(right))
    return (
        np.concatenate([into_h, into_l], axis=0),
        back.astype(jnp.bfloat16),
        turn,
        right_h,
        right_l,
        np.stack(left).astype(jnp.bfloat16),
    )


def dot(a, b):
    return jnp.dot(a, b, preferred_element_type=F32)


def small_dft(xs, sign):
    count = len(xs)
    if count == 1:
        return xs
    even = small_dft(xs[0::2], sign)
    odd = small_dft(xs[1::2], sign)
    out = [None] * count
    for k in range(count // 2):
        re, im = odd[k]
        angle = sign * 2 * np.pi * k / count
        c, s = float(np.cos(angle)), float(np.sin(angle))
        if k == 0:
            tr, ti = re, im
        elif 4 * k == count:
            tr, ti = (-im, re) if sign > 0 else (im, -re)
        else:
            tr, ti = re * c - im * s, re * s + im * c
        er, ei = even[k]
        out[k] = (er + tr, ei + ti)
        out[k + count // 2] = (er - tr, ei - ti)
    return out


def select(xs, lane, bit, hop):
    take = (lane // bit) % 2 == 1
    return [jnp.where(take, xs[(m + hop) % len(xs)], x) for m, x in enumerate(xs)]


def combine(xs, chunk, chunks, group):
    lane = lax.broadcasted_iota(jnp.int32, xs[0].shape, 1) // group
    shifts = [(part * chunks + chunk) * group for part in range(len(xs))]
    xs = [pltpu.roll(x, shift, 1) if shift else x for x, shift in zip(xs, shifts)]
    hop = 1
    while hop < len(xs):
        xs = select(xs, lane, hop * chunks, hop)
        hop *= 2
    return xs


def spread(xs, chunks, group, width):
    fold = len(xs)
    lane = lax.broadcasted_iota(jnp.int32, xs[0].shape, 1) // group
    bit = 1
    while bit < chunks:
        xs = select(xs, lane, bit, bit)
        bit *= 2
    xs = [xs[(fold - e) % fold] for e in range(fold)]
    return [pltpu.roll(x, width - e * group, 1) if e else x for e, x in enumerate(xs)]


def regroup(xs, fold, width):
    group = width // fold
    return spread(combine(xs, 0, 1, group), 1, group, width)


def body(
    parts, high, mid, fold, width,
    q_hbm, k_hbm, v_hbm, taps_hbm, bias_hbm, f_hbm, into_hbm, back_hbm, turn_hbm, right_h_hbm, right_l_hbm, left_hbm, o_hbm,
    o_ref, stored,
    taps, bias, q_in, k_in, v_in, f_in, into, back, turn, right_h, right_l, left, loaded,
    halo, mixed, q_feat, wide, out_f, out_m, out_y, in_f, in_m, in_y,
    mid_a, z_h, z_l, spectrum, gathered,
    send, recv, own, send_f, recv_f, own_f, halo_send, halo_recv,
):
    me = lax.axis_index("ctx")
    chunks = fold // parts
    first = parts * high
    block = mid * fold
    pitch = block + PAD
    length = high * block
    count = taps.shape[1]
    streams = (q_in, k_in, v_in)

    barrier = pltpu.get_barrier_semaphore()

    def greet(k, carry):
        pl.semaphore_signal(barrier, inc=1, device_id={"ctx": lax.rem(me + k, parts)}, device_id_type=MESH)
        return carry

    lax.fori_loop(1, parts, greet, 0)

    pairs = (
        (f_hbm, f_in), (k_hbm, k_in), (v_hbm, v_in), (q_hbm, q_in), (taps_hbm, taps), (bias_hbm, bias), (into_hbm, into), (turn_hbm, turn),
        (right_h_hbm, right_h), (right_l_hbm, right_l), (left_hbm, left), (back_hbm, back),
    )
    loads = [pltpu.make_async_copy(a, b, loaded.at[i]) for i, (a, b) in enumerate(pairs)]
    loads[0].start()

    def filter_copy(r, there, slot, source):
        return pltpu.make_async_remote_copy(
            src_ref=out_f.at[r, there],
            dst_ref=in_f.at[r, slot],
            send_sem=send_f.at[r, there],
            recv_sem=recv_f.at[r, source],
            device_id={"ctx": there},
            device_id_type=MESH,
        )

    outs = (out_m, out_y)
    ins = (in_m, in_y)

    def remote(kind, g, there, slot, source):
        return pltpu.make_async_remote_copy(
            src_ref=outs[kind].at[g, there],
            dst_ref=ins[kind].at[g, slot],
            send_sem=send.at[kind, g, there],
            recv_sem=recv.at[kind, g, source],
            device_id={"ctx": there},
            device_id_type=MESH,
        )

    half = parts // 2
    far = jnp.where(me < half, half, 0)
    leads = lax.rem(lax.axis_index("ch"), 2) == 1
    lead = jnp.where(leads, half + 1, half)
    one = jnp.where(leads, far, half - far)
    two = jnp.where(leads, half - far, far)

    def apart(go):
        def step(k, carry):
            go(jnp.where(k < lead, one, two) + lax.rem(me + k, half))
            return carry

        lax.fori_loop(1, parts, step, 0)

    def every(go):
        def step(k, carry):
            go(lax.rem(me + k, parts))
            return carry

        lax.fori_loop(1, parts, step, 0)

    def local_copy(kind, g):
        return pltpu.make_async_copy(outs[kind].at[g, me], ins[kind].at[g, me], own.at[kind, g])

    def local_filter(r):
        return pltpu.make_async_copy(out_f.at[r, me], in_f.at[r, me], own_f.at[r])

    def start(kind, g):
        every(lambda there: remote(kind, g, there, me, me).start())
        local_copy(kind, g).start()

    def wait(kind, g):
        every(lambda there: remote(kind, g, there, there, there).wait_recv())
        local_copy(kind, g).wait()

    def halo_copy(s):
        return pltpu.make_async_remote_copy(
            src_ref=streams[s].at[pl.ds(length - 16, 16)],
            dst_ref=halo.at[s],
            send_sem=halo_send.at[s],
            recv_sem=halo_recv.at[s],
            device_id={"ctx": lax.rem(me + 1, parts)},
            device_id_type=MESH,
        )

    rows = 64
    per_block = block // rows

    def wide_at(i):
        return pl.ds(pl.multiple_of((i // per_block) * pitch + (i % per_block) * rows, 8), rows)

    def rows_at(i):
        return pl.ds(pl.multiple_of(i * rows, rows), rows)

    tile = 16

    def pack_rows(r, store):
        def step(i, carry):
            xs = [wide[pl.ds(i * tile * pitch + r * fold + l, tile, stride=pitch), :] for l in range(fold)]
            store(pl.ds(pl.multiple_of(i * tile, tile), tile), regroup(xs, fold, width))
            return carry

        lax.fori_loop(0, high // tile, step, 0)

    loads[0].wait()
    for load in loads[1:]:
        load.start()

    def widen(i, carry):
        wide[wide_at(i), :] = f_in[rows_at(i), :].astype(F32)
        return carry

    lax.fori_loop(0, length // rows, widen, 0)

    def pack_filter(r, carry):
        def store(at, moved):
            for e in range(fold):
                out_f[r, e // chunks, e % chunks, at, :] = moved[e].astype(BF)

        pack_rows(r, store)
        return carry

    pack_filter(0, 0)
    pl.semaphore_wait(barrier, parts - 1)

    def send_filter(r, carry):
        apart(lambda there: filter_copy(r, there, me, me).start())
        local_filter(r).start()
        return carry

    send_filter(0, 0)

    def more_filter(r, carry):
        pack_filter(r, 0)
        return send_filter(r, 0)

    lax.fori_loop(1, mid, more_filter, 0)

    for load in loads[1:6]:
        load.wait()
    for s in range(3):
        halo_copy(s).start()
    for s in range(3):
        halo_copy(s).wait_recv()
    inside = jnp.where(me == 0, 0.0, 1.0).astype(F32)

    def shifted(x_ref, s, i, tail):
        now = x_ref[rows_at(i), :].astype(F32)
        extended = jnp.concatenate([tail, now], axis=0)
        total = taps[s, 0][None] * now
        for j in range(1, count):
            total = total + taps[s, j][None] * pltpu.roll(extended, j, 0)[8:]
        return total, now[rows - 8 :]

    tails = [halo[s].astype(F32)[8:] * inside for s in range(3)]

    def features(i, carry):
        key, key_tail = shifted(k_in, 1, i, carry[0])
        val, val_tail = shifted(v_in, 2, i, carry[1])
        product = (key * val).astype(BF)
        mixed[rows_at(i), :] = product
        wide[wide_at(i), :] = product.astype(F32)
        return key_tail, val_tail

    lax.fori_loop(0, length // rows, features, (tails[1], tails[2]))

    def pack_mixed(r, carry):
        def store(at, moved):
            for e in range(fold):
                out_m[e % chunks, e // chunks, r, at, :] = moved[e].astype(BF)

        pack_rows(r, store)
        return carry

    lax.fori_loop(0, mid, pack_mixed, 0)
    for g in range(chunks):
        start(0, g)

    def q_features(i, carry):
        total, tail = shifted(q_in, 0, i, carry)
        q_feat[rows_at(i), :] = total.astype(BF)
        return tail

    lax.fori_loop(0, length // rows, q_features, tails[0])

    def twist(i, carry):
        at = pl.ds(pl.multiple_of(i * tile, tile), tile)
        low = pl.ds(pl.multiple_of(first + i * tile, tile), tile)
        xs = []
        for r in range(mid):
            re = mid_a[at, r * width : (r + 1) * width]
            im = mid_a[low, r * width : (r + 1) * width]
            tr, ti = turn[r, 0, at, :], turn[r, 1, at, :]
            xs.append((re * tr - im * ti, re * ti + im * tr))
        for c, pair in enumerate(small_dft(xs, -1)):
            for e in range(2):
                high_part = pair[e].astype(BF)
                z_h[c, at, e * width : (e + 1) * width] = high_part
                z_l[c, at, e * width : (e + 1) * width] = (pair[e] - high_part.astype(F32)).astype(BF)
        return carry

    def untwist(i, carry):
        at = pl.ds(pl.multiple_of(i * tile, tile), tile)
        low = pl.ds(pl.multiple_of(first + i * tile, tile), tile)
        xs = [(gathered[c, at, 0:width], gathered[c, at, width:]) for c in range(mid)]
        for r, (re, im) in enumerate(small_dft(xs, 1)):
            tr, ti = turn[r, 0, at, :], turn[r, 1, at, :]
            z_l[r // 2, at, (r % 2) * width : (r % 2 + 1) * width] = (re * tr + im * ti).astype(BF)
            z_h[r // 2, at, (r % 2) * width : (r % 2 + 1) * width] = (im * tr - re * ti).astype(BF)
        return carry

    def forward(source):
        for p in range(mid // 2):
            x = jnp.concatenate([source(2 * p), source(2 * p + 1)], axis=1)
            t = dot(into[...], x)
            mid_a[:, 2 * p * width : (2 * p + 2) * width] = t[: 2 * first] + t[2 * first :]
        lax.fori_loop(0, first // tile, twist, 0, unroll=2)

    def fine(c):
        top = z_h[c]
        return dot(top, right_h[c]) + dot(top, right_l[c]) + dot(z_l[c], right_h[c])

    for load in loads[6:]:
        load.wait()

    def arrive_filter(r, carry):
        every(lambda there: filter_copy(r, there, there, there).wait_recv())
        local_filter(r).wait()
        return carry

    lax.fori_loop(0, mid, arrive_filter, 0)

    def filter_chunk(g, carry):
        forward(lambda r: in_f[r, :, g].reshape(first, width))
        for c in range(mid):
            spectrum[g, c] = fine(c)
        return carry

    lax.fori_loop(0, chunks, filter_chunk, 0)

    def chunk(g, carry):
        wait(0, g)
        forward(lambda r: in_m[g, :, r].reshape(first, width))
        for c in range(mid):
            x = fine(c)
            h = spectrum[g, c]
            xr, xi, hr, hi = x[:, :width], x[:, width:], h[:, :width], h[:, width:]
            product = jnp.concatenate([xr * hr - xi * hi, xr * hi + xi * hr], axis=1).astype(BF)
            gathered[c] = dot(product, left[c])
        lax.fori_loop(0, first // tile, untwist, 0, unroll=2)
        for p in range(mid // 2):
            y = dot(back[:, :first], z_l[p]) + dot(back[:, first:], z_h[p])
            y = y.astype(BF)
            for e in range(2):
                out_y[g, :, 2 * p + e] = y[:, e * width : (e + 1) * width].reshape(parts, high, width)
        start(1, g)
        return carry

    lax.fori_loop(0, chunks, chunk, 0)

    group = width // fold
    tiles = high // tile

    def ready(g):
        def step(i, carry):
            r, at = i // tiles, pl.ds(pl.multiple_of(i % tiles * tile, tile), tile)
            xs = [in_y[g, part, r, at, :].astype(F32) for part in range(parts)]
            for part, x in enumerate(combine(xs, g, chunks, group)):
                in_y[g, part, r, at, :] = x.astype(BF)
            return carry

        lax.fori_loop(0, mid * tiles, step, 0)

    for s in range(3):
        halo_copy(s).wait_send()

    def drain_filter(r, carry):
        every(lambda there: filter_copy(r, there, me, me).wait_send())
        return carry

    lax.fori_loop(0, mid, drain_filter, 0)

    def drain(g, carry):
        every(lambda there: remote(0, g, there, me, me).wait_send())
        return carry

    lax.fori_loop(0, chunks, drain, 0)

    for g in range(chunks - 1):
        wait(1, g)
        ready(g)
        every(lambda there: remote(1, g, there, me, me).wait_send())
    wait(1, chunks - 1)

    def unpack(i, carry):
        r, k = i // tiles, i % tiles
        at = pl.ds(pl.multiple_of(k * tile, tile), tile)
        fresh = [in_y[chunks - 1, part, r, at, :].astype(F32) for part in range(parts)]
        fresh = combine(fresh, chunks - 1, chunks, group)
        xs = [
            fresh[e // chunks] if e % chunks == chunks - 1 else in_y[e % chunks, e // chunks, r, at, :].astype(F32)
            for e in range(fold)
        ]
        for l, x in enumerate(spread(xs, chunks, group, width)):
            wide[pl.ds(k * tile * pitch + r * fold + l, tile, stride=pitch), :] = x
        return carry

    lax.fori_loop(0, mid * tiles, unpack, 0)

    def gate(i, carry):
        at = rows_at(i)
        total = wide[wide_at(i), :] + bias[...] * mixed[at, :].astype(F32)
        o_ref[at, :] = (q_feat[at, :].astype(F32) * total).astype(BF)
        return carry

    stores = []
    span = length // OUTS
    for k in range(OUTS):
        lax.fori_loop(k * span // rows, (k + 1) * span // rows, gate, 0, unroll=4)
        at = pl.ds(k * span, span)
        stores.append(pltpu.make_async_copy(o_ref.at[at], o_hbm.at[at], stored.at[k]))
        stores[k].start()

    every(lambda there: remote(1, chunks - 1, there, me, me).wait_send())
    for store in stores:
        store.wait()


def local(query, key_proj, value, short_taps, bias, long_filter):
    length, width = query.shape
    parts = lax.axis_size("ctx")
    chunks = max(1, min(CHUNKS, width // (4 * parts)))
    fold = parts * chunks
    high = max(16, 256 // parts)
    mid = length // (fold * high)
    first = parts * high
    tables = make_tables(parts, high, mid, fold, width)
    rows = pltpu.VMEM((length, width), BF)
    by_row = pltpu.VMEM((mid, parts, chunks, high, width), BF)
    by_chunk = pltpu.VMEM((chunks, parts, mid, high, width), BF)
    tall = pltpu.VMEM((mid, first, 2 * width), BF)
    hbm = pl.BlockSpec(memory_space=pl.ANY)
    return pl.pallas_call(
        functools.partial(body, parts, high, mid, fold, width),
        out_shape=jax.ShapeDtypeStruct((length, width), BF),
        in_specs=[hbm] * 12,
        out_specs=hbm,
        scratch_shapes=[
            rows,
            pltpu.SemaphoreType.DMA((OUTS,)),
            pltpu.VMEM(short_taps.shape, F32),
            pltpu.VMEM((1, width), F32),
            rows, rows, rows, rows,
            *[pltpu.VMEM(t.shape, t.dtype) for t in tables],
            pltpu.SemaphoreType.DMA((12,)),
            pltpu.VMEM((3, 16, width), BF),
            rows, rows,
            pltpu.VMEM((high * (mid * fold + PAD), width), F32),
            by_row, by_chunk, by_chunk, by_row, by_chunk, by_chunk,
            pltpu.VMEM((2 * first, mid * width), F32),
            tall, tall,
            pltpu.VMEM((chunks, mid, first, 2 * width), F32),
            pltpu.VMEM((mid, first, 2 * width), F32),
            pltpu.SemaphoreType.DMA((2, chunks, parts)),
            pltpu.SemaphoreType.DMA((2, chunks, parts)),
            pltpu.SemaphoreType.DMA((2, chunks)),
            pltpu.SemaphoreType.DMA((mid, parts)),
            pltpu.SemaphoreType.DMA((mid, parts)),
            pltpu.SemaphoreType.DMA((mid,)),
            pltpu.SemaphoreType.DMA((3,)),
            pltpu.SemaphoreType.DMA((3,)),
        ],
        compiler_params=pltpu.CompilerParams(
            vmem_limit_bytes=56 * 1024 * 1024, collective_id=0, has_side_effects=True
        ),
    )(query, key_proj, value, short_taps, bias.reshape(1, width), long_filter, *tables)


def solution(mesh):
    in_specs = (
        P("ctx", "ch"),
        P("ctx", "ch"),
        P("ctx", "ch"),
        P(None, None, "ch"),
        P("ch"),
        P("ctx", "ch"),
    )
    return jax.shard_map(local, mesh=mesh, in_specs=in_specs, out_specs=P("ctx", "ch"), check_vma=False)
```

```python
import functools

import jax
import jax.numpy as jnp
import numpy as np
from jax import lax
from jax.experimental import pallas as pl
from jax.experimental.pallas import tpu as pltpu
from jax.sharding import PartitionSpec as P

BF = jnp.bfloat16
F32 = jnp.float32
CHUNKS = 4
PAD = 8
OUTS = 2
MESH = pl.DeviceIdType.MESH


def halves(table):
    table = np.asarray(table, np.float32)
    high = table.astype(jnp.bfloat16)
    return high, (table - high.astype(np.float32)).astype(jnp.bfloat16)


def make_tables(parts, high, mid, fold, width):
    group = width // fold
    first = parts * high
    n = first * mid * fold
    s = np.arange(first)
    lane = np.arange(fold)
    angle = 2 * np.pi * ((np.outer(s, 4 * s + 1) % (4 * first)) / (4 * first))
    into = np.concatenate([np.cos(angle.T), -np.sin(angle.T)], axis=0)
    back = np.concatenate([np.cos(angle), -np.sin(angle)], axis=1) / n
    f = np.arange(mid)[:, None, None] * fold + np.repeat(lane, group)[None, None, :]
    turn = np.exp(-2j * np.pi * f * (s[None, :, None] + 0.25) / n)
    turn = np.stack([turn.real, turn.imag], axis=1).astype(np.float32)
    right, left = [], []
    for c in range(mid):
        w = np.exp(-2j * np.pi * (np.outer(lane, np.full(fold, c)) / (mid * fold) + np.outer(lane, lane) / fold))
        w = np.kron(w, np.eye(group))
        right.append(np.block([[w.real, w.imag], [-w.imag, w.real]]))
        v = w.conj().T
        left.append(np.block([[v.real, v.imag], [-v.imag, v.real]]))
    into_h, into_l = halves(into)
    right_h, right_l = halves(np.stack(right))
    return (
        np.concatenate([into_h, into_l], axis=0),
        back.astype(jnp.bfloat16),
        turn,
        right_h,
        right_l,
        np.stack(left).astype(jnp.bfloat16),
    )


def dot(a, b):
    return jnp.dot(a, b, preferred_element_type=F32)


def small_dft(xs, sign):
    count = len(xs)
    if count == 1:
        return xs
    even = small_dft(xs[0::2], sign)
    odd = small_dft(xs[1::2], sign)
    out = [None] * count
    for k in range(count // 2):
        re, im = odd[k]
        angle = sign * 2 * np.pi * k / count
        c, s = float(np.cos(angle)), float(np.sin(angle))
        if k == 0:
            tr, ti = re, im
        elif 4 * k == count:
            tr, ti = (-im, re) if sign > 0 else (im, -re)
        else:
            tr, ti = re * c - im * s, re * s + im * c
        er, ei = even[k]
        out[k] = (er + tr, ei + ti)
        out[k + count // 2] = (er - tr, ei - ti)
    return out


def select(xs, lane, bit, hop):
    take = (lane // bit) % 2 == 1
    return [jnp.where(take, xs[(m + hop) % len(xs)], x) for m, x in enumerate(xs)]


def combine(xs, chunk, chunks, group):
    lane = lax.broadcasted_iota(jnp.int32, xs[0].shape, 1) // group
    shifts = [(part * chunks + chunk) * group for part in range(len(xs))]
    xs = [pltpu.roll(x, shift, 1) if shift else x for x, shift in zip(xs, shifts)]
    hop = 1
    while hop < len(xs):
        xs = select(xs, lane, hop * chunks, hop)
        hop *= 2
    return xs


def spread(xs, chunks, group, width):
    fold = len(xs)
    lane = lax.broadcasted_iota(jnp.int32, xs[0].shape, 1) // group
    bit = 1
    while bit < chunks:
        xs = select(xs, lane, bit, bit)
        bit *= 2
    xs = [xs[(fold - e) % fold] for e in range(fold)]
    return [pltpu.roll(x, width - e * group, 1) if e else x for e, x in enumerate(xs)]


def regroup(xs, fold, width):
    group = width // fold
    return spread(combine(xs, 0, 1, group), 1, group, width)


def body(
    parts, high, mid, fold, width,
    q_hbm, k_hbm, v_hbm, taps_hbm, bias_hbm, f_hbm, into_hbm, back_hbm, turn_hbm, right_h_hbm, right_l_hbm, left_hbm, o_hbm,
    o_ref, stored,
    taps, bias, q_in, k_in, v_in, f_in, into, back, turn, right_h, right_l, left, loaded,
    halo, mixed, q_feat, wide, out_f, out_m, out_y, in_f, in_m, in_y,
    mid_a, z_h, z_l, spectrum, gathered,
    send, recv, own, send_f, recv_f, own_f, halo_send, halo_recv,
):
    me = lax.axis_index("ctx")
    chunks = fold // parts
    first = parts * high
    block = mid * fold
    pitch = block + PAD
    length = high * block
    count = taps.shape[1]
    streams = (q_in, k_in, v_in)

    barrier = pltpu.get_barrier_semaphore()

    def greet(k, carry):
        pl.semaphore_signal(barrier, inc=1, device_id={"ctx": lax.rem(me + k, parts)}, device_id_type=MESH)
        return carry

    lax.fori_loop(1, parts, greet, 0)

    pairs = (
        (f_hbm, f_in), (k_hbm, k_in), (v_hbm, v_in), (q_hbm, q_in), (taps_hbm, taps), (bias_hbm, bias), (into_hbm, into), (turn_hbm, turn),
        (right_h_hbm, right_h), (right_l_hbm, right_l), (left_hbm, left), (back_hbm, back),
    )
    loads = [pltpu.make_async_copy(a, b, loaded.at[i]) for i, (a, b) in enumerate(pairs)]
    loads[0].start()

    def filter_copy(r, there, slot, source):
        return pltpu.make_async_remote_copy(
            src_ref=out_f.at[r, there],
            dst_ref=in_f.at[r, slot],
            send_sem=send_f.at[r, there],
            recv_sem=recv_f.at[r, source],
            device_id={"ctx": there},
            device_id_type=MESH,
        )

    outs = (out_m, out_y)
    ins = (in_m, in_y)

    def remote(kind, g, there, slot, source):
        return pltpu.make_async_remote_copy(
            src_ref=outs[kind].at[g, there],
            dst_ref=ins[kind].at[g, slot],
            send_sem=send.at[kind, g, there],
            recv_sem=recv.at[kind, g, source],
            device_id={"ctx": there},
            device_id_type=MESH,
        )

    half = parts // 2
    far = jnp.where(me < half, half, 0)
    leads = lax.rem(lax.axis_index("ch"), 2) == 1
    lead = jnp.where(leads, half + 1, half)
    one = jnp.where(leads, far, half - far)
    two = jnp.where(leads, half - far, far)

    def apart(go):
        def step(k, carry):
            go(jnp.where(k < lead, one, two) + lax.rem(me + k, half))
            return carry

        lax.fori_loop(1, parts, step, 0)

    def every(go):
        def step(k, carry):
            go(lax.rem(me + k, parts))
            return carry

        lax.fori_loop(1, parts, step, 0)

    def local_copy(kind, g):
        return pltpu.make_async_copy(outs[kind].at[g, me], ins[kind].at[g, me], own.at[kind, g])

    def local_filter(r):
        return pltpu.make_async_copy(out_f.at[r, me], in_f.at[r, me], own_f.at[r])

    def start(kind, g):
        every(lambda there: remote(kind, g, there, me, me).start())
        local_copy(kind, g).start()

    def wait(kind, g):
        every(lambda there: remote(kind, g, there, there, there).wait_recv())
        local_copy(kind, g).wait()

    def halo_copy(s):
        return pltpu.make_async_remote_copy(
            src_ref=streams[s].at[pl.ds(length - 16, 16)],
            dst_ref=halo.at[s],
            send_sem=halo_send.at[s],
            recv_sem=halo_recv.at[s],
            device_id={"ctx": lax.rem(me + 1, parts)},
            device_id_type=MESH,
        )

    rows = 64
    per_block = block // rows

    def wide_at(i):
        return pl.ds(pl.multiple_of((i // per_block) * pitch + (i % per_block) * rows, 8), rows)

    def rows_at(i):
        return pl.ds(pl.multiple_of(i * rows, rows), rows)

    tile = 16

    def pack_rows(r, store):
        def step(i, carry):
            xs = [wide[pl.ds(i * tile * pitch + r * fold + l, tile, stride=pitch), :] for l in range(fold)]
            store(pl.ds(pl.multiple_of(i * tile, tile), tile), regroup(xs, fold, width))
            return carry

        lax.fori_loop(0, high // tile, step, 0)

    loads[0].wait()
    for load in loads[1:]:
        load.start()

    def widen(i, carry):
        wide[wide_at(i), :] = f_in[rows_at(i), :].astype(F32)
        return carry

    lax.fori_loop(0, length // rows, widen, 0)

    def pack_filter(r, carry):
        def store(at, moved):
            for e in range(fold):
                out_f[r, e // chunks, e % chunks, at, :] = moved[e].astype(BF)

        pack_rows(r, store)
        return carry

    pack_filter(0, 0)
    pl.semaphore_wait(barrier, parts - 1)

    def send_filter(r, carry):
        apart(lambda there: filter_copy(r, there, me, me).start())
        local_filter(r).start()
        return carry

    send_filter(0, 0)

    def more_filter(r, carry):
        pack_filter(r, 0)
        return send_filter(r, 0)

    lax.fori_loop(1, mid, more_filter, 0)

    for load in loads[1:6]:
        load.wait()
    for s in range(3):
        halo_copy(s).start()
    for s in range(3):
        halo_copy(s).wait_recv()
    inside = jnp.where(me == 0, 0.0, 1.0).astype(F32)

    def shifted(x_ref, s, i, tail):
        now = x_ref[rows_at(i), :].astype(F32)
        extended = jnp.concatenate([tail, now], axis=0)
        total = taps[s, 0][None] * now
        for j in range(1, count):
            total = total + taps[s, j][None] * pltpu.roll(extended, j, 0)[8:]
        return total, now[rows - 8 :]

    tails = [halo[s].astype(F32)[8:] * inside for s in range(3)]

    def features(i, carry):
        key, key_tail = shifted(k_in, 1, i, carry[0])
        val, val_tail = shifted(v_in, 2, i, carry[1])
        product = (key * val).astype(BF)
        mixed[rows_at(i), :] = product
        wide[wide_at(i), :] = product.astype(F32)
        return key_tail, val_tail

    lax.fori_loop(0, length // rows, features, (tails[1], tails[2]))

    def pack_mixed(r, carry):
        def store(at, moved):
            for e in range(fold):
                out_m[e % chunks, e // chunks, r, at, :] = moved[e].astype(BF)

        pack_rows(r, store)
        return carry

    lax.fori_loop(0, mid, pack_mixed, 0)
    for g in range(chunks):
        start(0, g)

    def q_features(i, carry):
        total, tail = shifted(q_in, 0, i, carry)
        q_feat[rows_at(i), :] = total.astype(BF)
        return tail

    lax.fori_loop(0, length // rows, q_features, tails[0])

    def twist(i, carry):
        at = pl.ds(pl.multiple_of(i * tile, tile), tile)
        low = pl.ds(pl.multiple_of(first + i * tile, tile), tile)
        xs = []
        for r in range(mid):
            re = mid_a[at, r * width : (r + 1) * width]
            im = mid_a[low, r * width : (r + 1) * width]
            tr, ti = turn[r, 0, at, :], turn[r, 1, at, :]
            xs.append((re * tr - im * ti, re * ti + im * tr))
        for c, pair in enumerate(small_dft(xs, -1)):
            for e in range(2):
                high_part = pair[e].astype(BF)
                z_h[c, at, e * width : (e + 1) * width] = high_part
                z_l[c, at, e * width : (e + 1) * width] = (pair[e] - high_part.astype(F32)).astype(BF)
        return carry

    def untwist(i, carry):
        at = pl.ds(pl.multiple_of(i * tile, tile), tile)
        low = pl.ds(pl.multiple_of(first + i * tile, tile), tile)
        xs = [(gathered[c, at, 0:width], gathered[c, at, width:]) for c in range(mid)]
        for r, (re, im) in enumerate(small_dft(xs, 1)):
            tr, ti = turn[r, 0, at, :], turn[r, 1, at, :]
            z_l[r // 2, at, (r % 2) * width : (r % 2 + 1) * width] = (re * tr + im * ti).astype(BF)
            z_h[r // 2, at, (r % 2) * width : (r % 2 + 1) * width] = (im * tr - re * ti).astype(BF)
        return carry

    def forward(source):
        for p in range(mid // 2):
            x = jnp.concatenate([source(2 * p), source(2 * p + 1)], axis=1)
            t = dot(into[...], x)
            mid_a[:, 2 * p * width : (2 * p + 2) * width] = t[: 2 * first] + t[2 * first :]
        lax.fori_loop(0, first // tile, twist, 0, unroll=2)

    def fine(c):
        top = z_h[c]
        return dot(top, right_h[c]) + dot(top, right_l[c]) + dot(z_l[c], right_h[c])

    for load in loads[6:]:
        load.wait()

    def arrive_filter(r, carry):
        every(lambda there: filter_copy(r, there, there, there).wait_recv())
        local_filter(r).wait()
        return carry

    lax.fori_loop(0, mid, arrive_filter, 0)

    def filter_chunk(g, carry):
        forward(lambda r: in_f[r, :, g].reshape(first, width))
        for c in range(mid):
            spectrum[g, c] = fine(c)
        return carry

    lax.fori_loop(0, chunks, filter_chunk, 0)

    def chunk(g, carry):
        wait(0, g)
        forward(lambda r: in_m[g, :, r].reshape(first, width))
        for c in range(mid):
            x = fine(c)
            h = spectrum[g, c]
            xr, xi, hr, hi = x[:, :width], x[:, width:], h[:, :width], h[:, width:]
            product = jnp.concatenate([xr * hr - xi * hi, xr * hi + xi * hr], axis=1).astype(BF)
            gathered[c] = dot(product, left[c])
        lax.fori_loop(0, first // tile, untwist, 0, unroll=2)
        for p in range(mid // 2):
            y = dot(back[:, :first], z_l[p]) + dot(back[:, first:], z_h[p])
            y = y.astype(BF)
            for e in range(2):
                out_y[g, :, 2 * p + e] = y[:, e * width : (e + 1) * width].reshape(parts, high, width)
        start(1, g)
        return carry

    lax.fori_loop(0, chunks, chunk, 0)

    group = width // fold
    tiles = high // tile

    def ready(g):
        def step(i, carry):
            r, at = i // tiles, pl.ds(pl.multiple_of(i % tiles * tile, tile), tile)
            xs = [in_y[g, part, r, at, :].astype(F32) for part in range(parts)]
            for part, x in enumerate(combine(xs, g, chunks, group)):
                in_y[g, part, r, at, :] = x.astype(BF)
            return carry

        lax.fori_loop(0, mid * tiles, step, 0)

    for s in range(3):
        halo_copy(s).wait_send()

    def drain_filter(r, carry):
        every(lambda there: filter_copy(r, there, me, me).wait_send())
        return carry

    lax.fori_loop(0, mid, drain_filter, 0)

    def drain(g, carry):
        every(lambda there: remote(0, g, there, me, me).wait_send())
        return carry

    lax.fori_loop(0, chunks, drain, 0)

    for g in range(chunks - 1):
        wait(1, g)
        ready(g)
        every(lambda there: remote(1, g, there, me, me).wait_send())
    wait(1, chunks - 1)

    def unpack(i, carry):
        r, k = i // tiles, i % tiles
        at = pl.ds(pl.multiple_of(k * tile, tile), tile)
        fresh = [in_y[chunks - 1, part, r, at, :].astype(F32) for part in range(parts)]
        fresh = combine(fresh, chunks - 1, chunks, group)
        xs = [
            fresh[e // chunks] if e % chunks == chunks - 1 else in_y[e % chunks, e // chunks, r, at, :].astype(F32)
            for e in range(fold)
        ]
        for l, x in enumerate(spread(xs, chunks, group, width)):
            wide[pl.ds(k * tile * pitch + r * fold + l, tile, stride=pitch), :] = x
        return carry

    lax.fori_loop(0, mid * tiles, unpack, 0)

    def gate(i, carry):
        at = rows_at(i)
        total = wide[wide_at(i), :] + bias[...] * mixed[at, :].astype(F32)
        o_ref[at, :] = (q_feat[at, :].astype(F32) * total).astype(BF)
        return carry

    stores = []
    span = length // OUTS
    for k in range(OUTS):
        lax.fori_loop(k * span // rows, (k + 1) * span // rows, gate, 0, unroll=4)
        at = pl.ds(k * span, span)
        stores.append(pltpu.make_async_copy(o_ref.at[at], o_hbm.at[at], stored.at[k]))
        stores[k].start()

    every(lambda there: remote(1, chunks - 1, there, me, me).wait_send())
    for store in stores:
        store.wait()


def local(query, key_proj, value, short_taps, bias, long_filter):
    length, width = query.shape
    parts = lax.axis_size("ctx")
    chunks = max(1, min(CHUNKS, width // (4 * parts)))
    fold = parts * chunks
    high = max(16, 256 // parts)
    mid = length // (fold * high)
    first = parts * high
    tables = make_tables(parts, high, mid, fold, width)
    rows = pltpu.VMEM((length, width), BF)
    by_row = pltpu.VMEM((mid, parts, chunks, high, width), BF)
    by_chunk = pltpu.VMEM((chunks, parts, mid, high, width), BF)
    tall = pltpu.VMEM((mid, first, 2 * width), BF)
    hbm = pl.BlockSpec(memory_space=pl.ANY)
    return pl.pallas_call(
        functools.partial(body, parts, high, mid, fold, width),
        out_shape=jax.ShapeDtypeStruct((length, width), BF),
        in_specs=[hbm] * 12,
        out_specs=hbm,
        scratch_shapes=[
            rows,
            pltpu.SemaphoreType.DMA((OUTS,)),
            pltpu.VMEM(short_taps.shape, F32),
            pltpu.VMEM((1, width), F32),
            rows, rows, rows, rows,
            *[pltpu.VMEM(t.shape, t.dtype) for t in tables],
            pltpu.SemaphoreType.DMA((12,)),
            pltpu.VMEM((3, 16, width), BF),
            rows, rows,
            pltpu.VMEM(((high + 1) * (mid * fold + PAD), width), F32),
            by_row, by_chunk, by_chunk, by_row, by_chunk, by_chunk,
            pltpu.VMEM((2 * first, mid * width), F32),
            tall, tall,
            pltpu.VMEM((chunks, mid, first, 2 * width), F32),
            pltpu.VMEM((mid, first, 2 * width), F32),
            pltpu.SemaphoreType.DMA((2, chunks, parts)),
            pltpu.SemaphoreType.DMA((2, chunks, parts)),
            pltpu.SemaphoreType.DMA((2, chunks)),
            pltpu.SemaphoreType.DMA((mid, parts)),
            pltpu.SemaphoreType.DMA((mid, parts)),
            pltpu.SemaphoreType.DMA((mid,)),
            pltpu.SemaphoreType.DMA((3,)),
            pltpu.SemaphoreType.DMA((3,)),
        ],
        compiler_params=pltpu.CompilerParams(
            vmem_limit_bytes=56 * 1024 * 1024, collective_id=0, has_side_effects=True
        ),
    )(query, key_proj, value, short_taps, bias.reshape(1, width), long_filter, *tables)


def solution(mesh):
    in_specs = (
        P("ctx", "ch"),
        P("ctx", "ch"),
        P("ctx", "ch"),
        P(None, None, "ch"),
        P("ch"),
        P("ctx", "ch"),
    )
    return jax.shard_map(local, mesh=mesh, in_specs=in_specs, out_specs=P("ctx", "ch"), check_vma=False)
```
